256 devices in a mesh: coil: 16 (over x_hi, y, core), slab: 16 (over x_lo, z).
Axes of the slice: x: 4 (x_hi: 2, x_lo: 2; x = x_hi * 2 + x_lo), y: 4, z: 8, core: 2. Of those that a mesh axis runs over, the one named last changes fastest.
Arguments:
- image: float32 [48, 2, 256, 256], P('coil', None, 'slab'), may hold values from -6 to 6
- sensitivity: bfloat16 [16, 48, 2, 256, 256], P('coil', None, None, 'slab'), may hold values from -1.1953125 to 1.1953125
- kspace: bfloat16 [16, 48, 2, 256, 256], P('coil', 'slab'), may hold values from -6 to 6
- sampling: int32 [256, 256], replicated, may hold values 0 or 1
- conv_in: bfloat16 [32, 2, 3, 3, 3], replicated, may hold values from -0.875 to 0.875
- conv_mid: bfloat16 [32, 32, 3, 3, 3], replicated, may hold values from -0.21875 to 0.21875
- conv_out: bfloat16 [2, 32, 3, 3, 3], replicated, may hold values from -0.21875 to 0.21875
Outputs:
- estimate: float32 [48, 2, 256, 256], P('coil', None, 'slab')
The draws below stay inside these ranges and needn't reach their ends.
All inputs are finite; a program needn't handle non-finite values.
Results may differ from the reference program's by a relative error of at most 0.015.
Values may be sent and summed in bfloat16 or wider, within the bound.
No kernel may reach another device: no remote copies, remote signals or barrier semaphores. Data moves between devices by JAX's collectives and lax.ppermute only.
A program may use at most 64 MiB of HBM per device.

```python
import math
import jax
import jax.numpy as jnp
from jax import lax

XR = 48
NY = 256
NZ = 256
NC = 16
HID = 32


def with_ends(array, rng, least, high):
    longest = array.shape.index(max(array.shape))
    spots = []
    for shift in (0, 1):
        where = [jax.random.randint(jax.random.fold_in(rng, axis), (), 0, length) for axis, length in enumerate(array.shape)]
        where[longest] = (where[longest] + shift) % array.shape[longest]
        spots.append(tuple(where))
    return array.at[spots[0]].set(least).at[spots[1]].set(high)


def with_spikes(result, rng, source, target, shards_of, factor):
    def block_of(axis_at):
        return (jnp.arange(result.shape[axis_at]) // (result.shape[axis_at] // shards_of)).reshape((-1,) + (1,) * (result.ndim - 1 - axis_at))

    near = jax.random.permutation(rng, shards_of)[block_of(target)]
    second = (block_of(target) + shards_of // 2) % shards_of
    return jnp.where((block_of(source) == near) | (block_of(source) == second), factor * result, result)


def level_of(key, shape, pieces, least, largest):
    factor_of, own = 1.0, jax.random.fold_in(key, 6)
    for position, shards_of in pieces:
        steps = jnp.exp(jax.random.uniform(jax.random.fold_in(own, position), (shards_of,), jnp.float32, least / len(pieces), largest / len(pieces)))
        factor_of = factor_of * jnp.repeat(steps, shape[position] // shards_of).reshape([-1 if axis == position else 1 for axis in range(len(shape))])
    return factor_of


def bell_draw(rng, dims, scale, most, shards=(), kind=jnp.bfloat16):
    entries = jax.random.normal(rng, dims, jnp.float32) * scale
    if len(shards) > 0:
        entries = level_of(rng, dims, shards, -0.22, 0.18) * entries
    return jnp.clip(entries, min=-most, max=most).astype(kind)


def gaussian_with(key, extent, spread, most, shards, heavy, held_as=jnp.bfloat16):
    entries = spread * jax.random.normal(key, extent, jnp.float32)
    if shards:
        entries = entries * level_of(key, extent, shards, -0.22, 0.18)
    return jnp.clip(with_spikes(entries, jax.random.fold_in(key, 3), *heavy), -most, most).astype(held_as)


def setup_inputs(seed: int = 0) -> dict:
    key_list = jax.random.split(jax.random.key(seed), 8)
    image = bell_draw(key_list[0], (XR, 2, NZ, NY), 1.0, 6.0, ((0, 16), (2, 16)), jnp.float32)
    sensitivity = gaussian_with(key_list[1], (NC, XR, 2, NZ, NY), 0.18, 1.1953125, ((0, 16), (3, 16)), (0, 1, 16, 2.0))
    kspace = bell_draw(key_list[2], (NC, XR, 2, NZ, NY), 1.0, 6.0, ((0, 16), (1, 16)))
    sampling = with_ends((jax.random.randint(key_list[3], (NZ, NY), 0, 4) < 1).astype(jnp.int32), jax.random.fold_in(key_list[3], 1), 0, 1)
    conv_in = bell_draw(key_list[4], (HID, 2, 3, 3, 3), 54 ** -0.5, 0.875)
    conv_mid = bell_draw(key_list[5], (HID, HID, 3, 3, 3), (27 * HID) ** -0.5, 0.21875)
    conv_out = bell_draw(key_list[6], (2, HID, 3, 3, 3), (27 * HID) ** -0.5, 0.21875)
    return dict(image=image, sensitivity=sensitivity, kspace=kspace, sampling=sampling, conv_in=conv_in, conv_mid=conv_mid, conv_out=conv_out)


def twiddle(length, sign):
    ramp = jnp.arange(length, dtype=jnp.int32)
    phases = ramp[:, None] * ramp[None, :] % length
    angles = phases.astype(jnp.float32) * (2.0 * math.pi / length)
    factor = 1.0 / math.sqrt(length)
    return jnp.concatenate([jnp.cos(angles) * factor, sign * jnp.sin(angles) * factor], axis=1).astype(jnp.bfloat16)

def settle(values):
    return lax.optimization_barrier(values.astype(jnp.bfloat16))

def transform_last(values, table):
    length = values.shape[-1]
    product = jnp.einsum('...czj,jk->...czk', values.astype(jnp.float32), table.astype(jnp.float32))
    real_part = product[..., 0, :, :length] - product[..., 1, :, length:]
    imag_part = product[..., 0, :, length:] + product[..., 1, :, :length]
    return jnp.stack([real_part, imag_part], axis=-3)

def transform_middle(values, table):
    length = values.shape[-2]
    product = jnp.einsum('...cjy,jk->...cky', values.astype(jnp.float32), table.astype(jnp.float32))
    real_part = product[..., 0, :length, :] - product[..., 1, length:, :]
    imag_part = product[..., 0, length:, :] + product[..., 1, :length, :]
    return jnp.stack([real_part, imag_part], axis=-3)

def times_map(maps, field):
    real_part = maps[..., 0, :, :] * field[..., 0, :, :] - maps[..., 1, :, :] * field[..., 1, :, :]
    imag_part = maps[..., 0, :, :] * field[..., 1, :, :] + maps[..., 1, :, :] * field[..., 0, :, :]
    return jnp.stack([real_part, imag_part], axis=-3)

def times_conj(maps, field):
    real_part = maps[..., 0, :, :] * field[..., 0, :, :] + maps[..., 1, :, :] * field[..., 1, :, :]
    imag_part = maps[..., 0, :, :] * field[..., 1, :, :] - maps[..., 1, :, :] * field[..., 0, :, :]
    return jnp.stack([real_part, imag_part], axis=-3)

def convolve(values, weights):
    return lax.conv_general_dilated(values[None].astype(jnp.float32), weights.astype(jnp.float32), (1, 1, 1), ((1, 1), (1, 1), (1, 1)), dimension_numbers=('NDCHW', 'OIDHW', 'NDCHW'))[0]

def reference(image, sensitivity, kspace, sampling, conv_in, conv_mid, conv_out):
    rounded = settle(image).astype(jnp.float32)
    forward_y = twiddle(NY, -1.0)
    forward_z = twiddle(NZ, -1.0)
    back_z = twiddle(NZ, 1.0)
    back_y = twiddle(NY, 1.0)
    keep = sampling.astype(jnp.float32)

    def one_coil(total, pair):
        maps = pair[0].astype(jnp.float32)
        measured = pair[1].astype(jnp.float32)
        coil_image = settle(times_map(maps, rounded))
        lines = settle(transform_last(coil_image, forward_y))
        spectrum = transform_middle(lines, forward_z)
        misfit = settle(keep * (spectrum - measured))
        returned = settle(transform_middle(misfit, back_z))
        field = transform_last(returned, back_y)
        return (total + times_conj(maps, field), None)
    gradient, _ = lax.scan(one_coil, jnp.zeros(image.shape, jnp.float32), (sensitivity, kspace))
    halfway = image - gradient
    start = settle(halfway)
    first = settle(jax.nn.relu(convolve(start, conv_in)))
    second = settle(jax.nn.relu(convolve(first, conv_mid)))
    return halfway + convolve(second, conv_out)
```

```python
import math

import jax
import jax.numpy as jnp
import numpy as np
from jax import lax
from jax.experimental import pallas as pl
from jax.experimental.pallas import tpu as pltpu
from jax.sharding import PartitionSpec as P

BF16 = jnp.bfloat16
F32 = jnp.float32
WIN = 24
VMEM = pl.BlockSpec(memory_space=pltpu.VMEM)
SMEM = pl.BlockSpec(memory_space=pltpu.SMEM)


def tables(length):
    ramp = np.arange(length)
    angles = (ramp[:, None] * ramp[None, :] % length) * (2.0 * math.pi / length)
    re = np.cos(angles) / math.sqrt(length)
    im = -np.sin(angles) / math.sqrt(length)
    full = np.block([[re, im], [-im, re]])
    return jnp.asarray(full, BF16), jnp.asarray(full.T, BF16)


def dot(a, b):
    return jnp.dot(a, b, preferred_element_type=F32)


def coil_kernel(place_ref, sens_ref, img_a_ref, img_b_ref, ksp_ref, keep_ref, fwd_ref, bwd_ref,
                keep_out, send_out, pad_ref):
    n = ksp_ref.shape[-1]
    pairs = img_a_ref.shape[0]
    even_here, slot, turn = (place_ref[3] == 0, place_ref[4], place_ref[5])

    def image_part(p):
        planes = []
        for i in range(pairs):
            a, b = (img_a_ref[i ^ slot, 0, p], img_b_ref[i ^ slot, 0, p])
            planes += [jnp.where(even_here, a, b), jnp.where(even_here, b, a)]
        return jnp.concatenate(planes, axis=0).astype(F32)

    sr = sens_ref[:, 0, 0].reshape(n, n).astype(F32)
    si = sens_ref[:, 0, 1].reshape(n, n).astype(F32)
    mr, mi = (image_part(0), image_part(1))
    coil = jnp.concatenate([sr * mr - si * mi, sr * mi + si * mr], axis=1).astype(BF16)
    fwd, bwd = (fwd_ref[...], bwd_ref[...])
    lines = dot(coil, fwd).astype(BF16)
    lines = jnp.concatenate([lines[:, :n], lines[:, n:]], axis=0)
    spectrum = dot(bwd, lines)
    keep = jnp.concatenate([keep_ref[...]] * 2, axis=0).astype(F32)
    misfit = (keep * (spectrum - ksp_ref[0].reshape(2 * n, n).astype(F32))).astype(BF16)
    back = dot(fwd, misfit).astype(BF16)
    back = jnp.concatenate([back[:n], back[n:]], axis=1)
    field = dot(back, bwd)
    fr, fi = (field[:, :n], field[:, n:])
    sr = sens_ref[:, 0, 0].reshape(n, n).astype(F32)
    si = sens_ref[:, 0, 1].reshape(n, n).astype(F32)
    edge = jnp.zeros((8, n), F32)
    for p in range(2):
        pad_ref[p, 0:8] = edge
        pad_ref[p, n + 8 : n + 16] = edge
    pad_ref[0, 8 : n + 8] = sr * fr + si * fi
    pad_ref[1, 8 : n + 8] = sr * fi - si * fr
    depth = n // (2 * pairs)

    def window(j):
        at = j * depth + 4
        return jnp.concatenate([pad_ref[p, at : at + WIN] for p in range(2)], axis=0).astype(BF16)

    for i in range(pairs):
        even, odd = (window(2 * i), window(2 * i + 1))
        keep_out[i ^ turn, 0] = jnp.where(even_here, even, odd)
        send_out[i ^ turn, 0] = jnp.where(even_here, odd, even)


def coil_terms(place, sens, img_a, img_b, ksp, keep, fwd, bwd):
    slabs, rows, parts, depth, n = sens.shape
    pairs = img_a.shape[0]
    out = jax.ShapeDtypeStruct((pairs, rows, 2 * WIN, n), BF16)
    whole = lambda x: (0, 0)
    brick = lambda count: pl.BlockSpec((count, 1, parts, depth, n), lambda x: (0, x, 0, 0, 0))
    out_spec = pl.BlockSpec((pairs, 1, 2 * WIN, n), lambda x: (0, x, 0, 0))
    return pl.pallas_call(
        coil_kernel,
        grid=(rows,),
        in_specs=[
            SMEM,
            brick(slabs),
            brick(pairs),
            brick(pairs),
            pl.BlockSpec((1, parts, n, n), lambda x: (x, 0, 0, 0)),
            pl.BlockSpec((n, n), whole),
            pl.BlockSpec((2 * n, 2 * n), whole),
            pl.BlockSpec((2 * n, 2 * n), whole),
        ],
        out_specs=[out_spec, out_spec],
        out_shape=[out, out],
        scratch_shapes=[pltpu.VMEM((2, n + 16, n), F32)],
        compiler_params=pltpu.CompilerParams(vmem_limit_bytes=40 << 20),
        cost_estimate=pl.CostEstimate(
            flops=rows * 16 * 2 * n * n * n, bytes_accessed=6 << 20, transcendentals=0
        ),
        name="coil_terms",
    )(place, sens, img_a, img_b, ksp, keep, fwd, bwd)


def pair_kernel(a_ref, b_ref, out_ref):
    out_ref[...] = (a_ref[...].astype(F32) + b_ref[...].astype(F32)).astype(BF16)


def pair_sum(a, b):
    return pl.pallas_call(
        pair_kernel,
        in_specs=[VMEM, VMEM],
        out_specs=VMEM,
        out_shape=jax.ShapeDtypeStruct(a.shape, a.dtype),
        compiler_params=pltpu.CompilerParams(vmem_limit_bytes=16 << 20),
        name="pair_sum",
    )(a, b)


def start_kernel(place_ref, terms_ref, img_a_ref, img_b_ref, out_ref):
    pairs, rows = (terms_ref.shape[0], terms_ref.shape[1])
    plane, slot = (place_ref[2], place_ref[4])
    low_pair = jnp.maximum(plane - 1, 0) // 2
    high_pair = jnp.minimum(plane + 1, 2 * pairs - 1) // 2
    low_ok = jnp.where(plane > 0, 1.0, 0.0).astype(F32)
    high_ok = jnp.where(plane < 2 * pairs - 1, 1.0, 0.0).astype(F32)
    depth = img_a_ref.shape[3]
    for x in range(rows):
        total = terms_ref[0, x].astype(F32)
        for k in range(1, pairs):
            total += terms_ref[k, x].astype(F32)
        pieces = []
        for p in range(2):
            low = img_b_ref[low_pair ^ slot, x, p].astype(F32)[depth - 8 :] * low_ok
            own = img_a_ref[0, x, p].astype(F32)
            high = img_b_ref[high_pair ^ slot, x, p].astype(F32)[:8] * high_ok
            pieces.append(jnp.concatenate([low, own, high], axis=0)[4 : 4 + WIN])
        out_ref[x] = (jnp.concatenate(pieces, axis=0) - total).astype(BF16)


def start_brick(place, terms, img_a, img_b):
    _, rows, height, n = terms.shape
    return pl.pallas_call(
        start_kernel,
        in_specs=[SMEM, VMEM, VMEM, VMEM],
        out_specs=VMEM,
        out_shape=jax.ShapeDtypeStruct((rows, height, n), BF16),
        compiler_params=pltpu.CompilerParams(vmem_limit_bytes=16 << 20),
        name="start_brick",
    )(place, terms, img_a, img_b)


def shifted(value, column):
    n = value.shape[1]
    before = jnp.where(column == 0, 0.0, pltpu.roll(value, 1, 1))
    after = jnp.where(column == n - 1, 0.0, pltpu.roll(value, n - 1, 1))
    return before, value, after


def conv_kernel(place_ref, low_ref, own_ref, high_ref, w1_ref, w2_ref, w3_ref, out_ref,
                cols_ref, a1_ref, a2_ref):
    rows, height, n = own_ref.shape
    hid = 32
    ext = 3 * rows
    coil, slab = (place_ref[0], place_ref[1])
    flag = lambda ok: jnp.where(ok, 1.0, 0.0).astype(F32)
    x_low, x_high = (flag(coil > 0), flag(coil < pl.cdiv(48, rows) - 1))
    z_low, z_high = (flag(slab > 0), flag(slab < pl.cdiv(256, 16) - 1))

    for x in range(ext):
        src = (low_ref, own_ref, high_ref)[x // rows]
        value = src[x % rows].astype(F32)
        column = lax.broadcasted_iota(jnp.int32, value.shape, 1)
        for d, part in enumerate(shifted(value, column)):
            at = (x * 3 + d) * height
            cols_ref[at : at + height] = part.astype(BF16)

    column1 = lax.broadcasted_iota(jnp.int32, (w1_ref.shape[0], n), 1)
    w1 = w1_ref[:, : 9 * height]
    for x in range(ext - 2):
        at = x * 3 * height
        value = jnp.maximum(dot(w1, cols_ref[at : at + 9 * height]), 0.0)
        if x < rows - 1:
            value = value * x_low
        if x >= 2 * rows - 1:
            value = value * x_high
        value = jnp.concatenate(
            [value[: 2 * hid] * z_low, value[2 * hid : -2 * hid], value[-2 * hid :] * z_high], axis=0
        )
        for d, part in enumerate(shifted(value, column1)):
            a1_ref[x, d] = part.astype(BF16)

    blocks = 3
    out2 = 6 * hid
    for k in range(blocks):
        parts = {}
        for x in range(ext - 2):
            first = 0 if x <= ext - 5 else x - (ext - 5)
            last = min(x, 2)
            cols = jnp.concatenate([a1_ref[x, d, k * out2 : k * out2 + 256] for d in range(3)], axis=0)
            value = dot(w2_ref[first * out2 : (last + 1) * out2], cols)
            for dx in range(first, last + 1):
                piece = value[(dx - first) * out2 : (dx - first + 1) * out2]
                at = x - dx
                parts[at] = piece if at not in parts else parts[at] + piece
            done = x - 2
            if done >= 0:
                value = jnp.maximum(parts.pop(done), 0.0)
                if done < rows - 2:
                    value = value * x_low
                if done >= 2 * rows - 2:
                    value = value * x_high
                if k == 0:
                    value = jnp.concatenate([value[:hid] * z_low, value[hid:]], axis=0)
                if k == blocks - 1:
                    value = jnp.concatenate([value[:-hid], value[-hid:] * z_high], axis=0)
                a2_ref[done, k * out2 : (k + 1) * out2] = value.astype(BF16)

    depth = 16
    size = 2 * depth
    w3 = w3_ref[:, :576]
    terms = [dot(w3, a2_ref[x]) for x in range(rows + 2)]
    column3 = lax.broadcasted_iota(jnp.int32, (size, n), 1)
    for x in range(rows):
        sums = []
        for d in range(3):
            at = lambda dx: (dx * 3 + d) * size
            sums.append(sum(terms[x + dx][at(dx) : at(dx) + size] for dx in range(3)))
        value = sums[1] + jnp.where(column3 == 0, 0.0, pltpu.roll(sums[0], 1, 1))
        value = value + jnp.where(column3 == n - 1, 0.0, pltpu.roll(sums[2], n - 1, 1))
        half = own_ref[x].astype(F32)
        for p in range(2):
            mine = half[p * WIN + 4 : p * WIN + 4 + depth]
            out_ref[x, p] = mine + value[p * depth : (p + 1) * depth]


def regularized(place, low, own, high, w1, w2, w3, depth):
    rows, height, n = own.shape
    ext = 3 * rows
    return pl.pallas_call(
        conv_kernel,
        in_specs=[SMEM] + [VMEM] * 6,
        out_specs=VMEM,
        out_shape=jax.ShapeDtypeStruct((rows, 2, depth, n), F32),
        scratch_shapes=[
            pltpu.VMEM((ext * 3 * height, n), BF16),
            pltpu.VMEM((ext - 2, 3, 640, n), BF16),
            pltpu.VMEM((ext - 4, 576, n), BF16),
        ],
        compiler_params=pltpu.CompilerParams(vmem_limit_bytes=40 << 20),
        cost_estimate=pl.CostEstimate(flops=6 << 30, bytes_accessed=4 << 20, transcendentals=0),
        name="regularized",
    )(place, low, own, high, w1, w2, w3)


def weights_kernel(b1_ref, b2_ref, b3_ref, keep_ref, fwd_ref, bwd_ref,
                   w1_ref, w2_ref, w3_ref, keep_out, fwd_out, bwd_out):
    keep_out[...] = keep_ref[...].astype(F32).astype(BF16)
    fwd_out[...] = fwd_ref[...]
    bwd_out[...] = bwd_ref[...]
    base = b1_ref[...].astype(F32)
    for a in range(20):
        moved = base if a == 0 else pltpu.roll(base, a, 1)
        w1_ref[a * 32 : (a + 1) * 32] = moved.astype(BF16)
    for dx in range(3):
        for dy in range(3):
            base = b2_ref[dx * 3 + dy].astype(F32)
            for a in range(6):
                moved = base if a == 0 else pltpu.roll(base, a * 32, 1)
                at = (dx * 6 + a) * 32
                w2_ref[at : at + 32, dy * 256 : (dy + 1) * 256] = moved.astype(BF16)
    base = b3_ref[...].astype(F32)
    for t in range(18):
        row = jnp.broadcast_to(base[t : t + 1], (16, base.shape[1]))
        moved = pltpu.roll(row, 0, 1, stride=16, stride_axis=0)
        moved = pltpu.roll(moved, 0, 1, stride=16, stride_axis=0)
        w3_ref[t * 16 : (t + 1) * 16] = moved.astype(BF16)


def banded_weights(conv_in, conv_mid, conv_out, keep, fwd, bwd):
    b1 = jnp.pad(conv_in.transpose(0, 2, 4, 1, 3), ((0, 0),) * 4 + ((1, WIN - 4),))
    b1 = jnp.pad(b1.reshape(32, 18 * WIN), ((0, 0), (0, 512 - 18 * WIN)))
    b2 = conv_mid.transpose(2, 4, 0, 3, 1).reshape(9, 32, 96)
    b2 = jnp.pad(b2, ((0, 0), (0, 0), (0, 160)))
    b3 = conv_out.transpose(2, 4, 0, 3, 1).reshape(18, 96)
    b3 = jnp.pad(b3, ((0, 0), (0, 640 - 96)))
    return pl.pallas_call(
        weights_kernel,
        in_specs=[VMEM] * 6,
        out_specs=[VMEM] * 6,
        out_shape=[
            jax.ShapeDtypeStruct((640, 512), BF16),
            jax.ShapeDtypeStruct((576, 768), BF16),
            jax.ShapeDtypeStruct((288, 640), BF16),
            jax.ShapeDtypeStruct(keep.shape, BF16),
            jax.ShapeDtypeStruct(fwd.shape, BF16),
            jax.ShapeDtypeStruct(bwd.shape, BF16),
        ],
        compiler_params=pltpu.CompilerParams(vmem_limit_bytes=16 << 20),
        name="banded_weights",
    )(b1, b2, b3, keep, fwd, bwd)


def gathered(brick, chips):
    held = brick[None]
    for k in (4, 2, 1):
        came = lax.ppermute(held, "coil", [(i, i ^ (2 * k)) for i in range(2 * chips)])
        held = jnp.stack([held, came], axis=1).reshape(-1, *brick.shape)
    return held


def step(image, sensitivity, kspace, sampling, conv_in, conv_mid, conv_out):
    rows, parts, depth, n = image.shape
    coils, slabs = (lax.axis_size("coil"), lax.axis_size("slab"))
    coil, slab = (lax.axis_index("coil"), lax.axis_index("slab"))
    place = jnp.stack(
        [coil, slab, coil ^ slab, (coil ^ slab) % 2, (coil ^ slab) // 2, slab // 2]
    ).astype(jnp.int32)
    pairs = coils // 2
    chips = [[2 * i + c for i in range(pairs)] for c in range(2)]
    partner = [(i, i ^ 1) for i in range(coils)]
    across = [(a * slabs + b, (a ^ b) * slabs + a) for a in range(coils) for b in range(slabs)]
    w1, w2, w3, keep, fwd, bwd = banded_weights(
        conv_in, conv_mid, conv_out, sampling, *tables(n)
    )

    brick = lax.ppermute(image.astype(BF16), ("coil", "slab"), across)
    sens = lax.all_to_all(
        sensitivity[0].reshape(slabs, rows, parts, depth, n), "slab", 0, 0, tiled=True
    )
    img_a = gathered(brick, pairs)
    img_b = lax.ppermute(img_a, "coil", partner)

    kept, sent = coil_terms(place, sens, img_a, img_b, kspace[0], keep, fwd, bwd)
    terms = pair_sum(kept, lax.ppermute(sent, "coil", partner))
    terms = lax.all_to_all(terms, "coil", 0, 0, tiled=True, axis_index_groups=chips)
    start = start_brick(place, terms, img_a, img_b)

    def to(step):
        return [
            ((a ^ b) * slabs + a, (a + step) * slabs + b)
            for a in range(coils) for b in range(slabs) if 0 <= a + step < coils
        ]

    own = lax.ppermute(start, ("coil", "slab"), to(0))
    low = lax.ppermute(start, ("coil", "slab"), to(1))
    high = lax.ppermute(start, ("coil", "slab"), to(-1))
    return regularized(place, low, own, high, w1, w2, w3, depth)


def solution(mesh):
    return jax.shard_map(
        step,
        mesh=mesh,
        in_specs=(
            P("coil", None, "slab", None),
            P("coil", None, None, "slab", None),
            P("coil", "slab", None, None, None),
            P(),
            P(),
            P(),
            P(),
        ),
        out_specs=P("coil", None, "slab", None),
        check_vma=False,
    )
```

```python
import math

import jax
import jax.numpy as jnp
import numpy as np
from jax import lax
from jax.experimental import pallas as pl
from jax.experimental.pallas import tpu as pltpu
from jax.sharding import PartitionSpec as P

BF16 = jnp.bfloat16
F32 = jnp.float32
WIN = 24
VMEM = pl.BlockSpec(memory_space=pltpu.VMEM)
SMEM = pl.BlockSpec(memory_space=pltpu.SMEM)


def table(length):
    ramp = np.arange(length)
    angles = (ramp[:, None] * ramp[None, :] % length) * (2.0 * math.pi / length)
    re = np.cos(angles) / math.sqrt(length)
    im = -np.sin(angles) / math.sqrt(length)
    return jnp.asarray(np.concatenate([re, im, -im], axis=1), BF16)


def chip_of(z, slab):
    step = (0x72301456 >> (4 * ((z - slab) & 7))) & 7
    return ((slab >> 3) ^ (step >> 2)) * 4 + (((slab >> 1) + step) & 3)


def plane_of(coil, slab):
    chip = coil >> 1
    step = ((chip >> 2) ^ (slab >> 3)) * 4 + ((chip - (slab >> 1)) & 3)
    return (coil & 1) * 8 + ((slab + ((0x70125634 >> (4 * step)) & 7)) & 7)


def coil_of(plane, slab):
    return 2 * chip_of(plane & 7, slab) + (plane >> 3)


def dot(a, b):
    return jnp.dot(a, b, preferred_element_type=F32)


def coil_kernel(place_ref, sens_ref, img_a_ref, img_b_ref, ksp_ref, keep_ref, table_ref,
                keep_out, send_out, pad_ref):
    rows, n = (ksp_ref.shape[0], ksp_ref.shape[-1])
    half = img_a_ref.shape[0]
    coil, slab = (place_ref[0], place_ref[1])
    chip, low_half = (coil >> 1, (coil & 1) == 0)
    at = [chip_of(z, slab) for z in range(half)]

    def image_part(x, p):
        a = jnp.concatenate([img_a_ref[chip ^ at[z], x, p] for z in range(half)], axis=0)
        b = jnp.concatenate([img_b_ref[chip ^ at[z], x, p] for z in range(half)], axis=0)
        low, high = (jnp.where(low_half, a, b), jnp.where(low_half, b, a))
        return jnp.concatenate([low, high], axis=0).astype(F32)

    re, im, mi = (table_ref[:, i * n : (i + 1) * n] for i in range(3))
    fwd = jnp.concatenate([jnp.concatenate([re, im], axis=1), jnp.concatenate([mi, re], axis=1)], axis=0)
    bwd = jnp.concatenate([jnp.concatenate([re, mi], axis=1), jnp.concatenate([im, re], axis=1)], axis=0)
    keep = keep_ref[...].astype(F32)
    keep = jnp.concatenate([keep, keep], axis=0)
    edge = jnp.zeros((8, n), F32)
    depth = n // (2 * half)
    for x in range(rows):
        sr = sens_ref[:, x, 0].reshape(n, n).astype(F32)
        si = sens_ref[:, x, 1].reshape(n, n).astype(F32)
        mr, mi = (image_part(x, 0), image_part(x, 1))
        coil_image = jnp.concatenate([sr * mr - si * mi, sr * mi + si * mr], axis=1).astype(BF16)
        lines = dot(coil_image, fwd).astype(BF16)
        lines = jnp.concatenate([lines[:, :n], lines[:, n:]], axis=0)
        spectrum = dot(bwd, lines)
        misfit = (keep * (spectrum - ksp_ref[x].reshape(2 * n, n).astype(F32))).astype(BF16)
        back = dot(fwd, misfit).astype(BF16)
        back = jnp.concatenate([back[:n], back[n:]], axis=1)
        field = dot(back, bwd)
        fr, fi = (field[:, :n], field[:, n:])
        sr = sens_ref[:, x, 0].reshape(n, n).astype(F32)
        si = sens_ref[:, x, 1].reshape(n, n).astype(F32)
        for p in range(2):
            pad_ref[x, p, 0:8] = edge
            pad_ref[x, p, n + 8 : n + 16] = edge
        pad_ref[x, 0, 8 : n + 8] = sr * fr + si * fi
        pad_ref[x, 1, 8 : n + 8] = sr * fi - si * fr

        def window(j):
            first = j * depth + 4
            parts = [pad_ref[x, p, first : first + WIN] for p in range(2)]
            return jnp.concatenate(parts, axis=0).astype(BF16)

        for z in range(half):
            low, high = (window(z), window(half + z))
            keep_out[at[z], x] = jnp.where(low_half, low, high)
            send_out[at[z], x] = jnp.where(low_half, high, low)


def coil_terms(place, sens, img_a, img_b, ksp, keep, table):
    _, rows, _, _, n = sens.shape
    out = jax.ShapeDtypeStruct((img_a.shape[0], rows, 2 * WIN, n), BF16)
    return pl.pallas_call(
        coil_kernel,
        in_specs=[SMEM] + [VMEM] * 6,
        out_specs=[VMEM, VMEM],
        out_shape=[out, out],
        scratch_shapes=[pltpu.VMEM((rows, 2, n + 16, n), F32)],
        compiler_params=pltpu.CompilerParams(vmem_limit_bytes=40 << 20),
        cost_estimate=pl.CostEstimate(
            flops=rows * 16 * 2 * n * n * n, bytes_accessed=6 << 20, transcendentals=0
        ),
        name="coil_terms",
    )(place, sens, img_a, img_b, ksp, keep, table)


def pair_kernel(a_ref, b_ref, out_ref):
    out_ref[...] = a_ref[...] + b_ref[...]


def pair_sum(a, b):
    return pl.pallas_call(
        pair_kernel,
        in_specs=[VMEM, VMEM],
        out_specs=VMEM,
        out_shape=jax.ShapeDtypeStruct(a.shape, a.dtype),
        compiler_params=pltpu.CompilerParams(vmem_limit_bytes=16 << 20),
        name="pair_sum",
    )(a, b)


def start_kernel(place_ref, terms_ref, img_a_ref, img_b_ref, out_ref):
    pairs, rows = (terms_ref.shape[0], terms_ref.shape[1])
    coil, slab, plane = (place_ref[0], place_ref[1], place_ref[2])
    chip, half = (coil >> 1, coil & 1)
    below, above = (jnp.maximum(plane - 1, 0), jnp.minimum(plane + 1, 2 * pairs - 1))
    low_ok = jnp.where(plane > 0, 1.0, 0.0).astype(F32)
    high_ok = jnp.where(plane < 2 * pairs - 1, 1.0, 0.0).astype(F32)

    def brick(j, x, p):
        slot = chip ^ chip_of(j & 7, slab)
        value = jnp.where((j >> 3) == half, img_a_ref[slot, x, p], img_b_ref[slot, x, p])
        return value.astype(F32)

    depth = img_a_ref.shape[3]
    for x in range(rows):
        total = terms_ref[0, x].astype(F32)
        for k in range(1, pairs):
            total += terms_ref[k, x].astype(F32)
        pieces = []
        for p in range(2):
            low = brick(below, x, p)[depth - 8 :] * low_ok
            own = img_a_ref[0, x, p].astype(F32)
            high = brick(above, x, p)[:8] * high_ok
            pieces.append(jnp.concatenate([low, own, high], axis=0)[4 : 4 + WIN])
        out_ref[x] = (jnp.concatenate(pieces, axis=0) - total).astype(BF16)


def start_brick(place, terms, img_a, img_b):
    _, rows, height, n = terms.shape
    return pl.pallas_call(
        start_kernel,
        in_specs=[SMEM, VMEM, VMEM, VMEM],
        out_specs=VMEM,
        out_shape=jax.ShapeDtypeStruct((rows, height, n), BF16),
        compiler_params=pltpu.CompilerParams(vmem_limit_bytes=16 << 20),
        name="start_brick",
    )(place, terms, img_a, img_b)


def shifted(value, column):
    n = value.shape[1]
    before = jnp.where(column == 0, 0.0, pltpu.roll(value, 1, 1))
    after = jnp.where(column == n - 1, 0.0, pltpu.roll(value, n - 1, 1))
    return before, value, after


def conv_kernel(place_ref, low_ref, own_ref, high_ref, w1_ref, w2_ref, w3_ref, out_ref,
                cols_ref, a1_ref, a2_ref):
    rows, height, n = own_ref.shape
    hid = 32
    ext = 3 * rows
    coil, slab = (place_ref[0], place_ref[1])
    flag = lambda ok: jnp.where(ok, 1.0, 0.0).astype(F32)
    x_low, x_high = (flag(coil > 0), flag(coil < pl.cdiv(48, rows) - 1))
    z_low, z_high = (flag(slab > 0), flag(slab < pl.cdiv(256, 16) - 1))

    for x in range(ext):
        src = (low_ref, own_ref, high_ref)[x // rows]
        value = src[x % rows].astype(F32)
        column = lax.broadcasted_iota(jnp.int32, value.shape, 1)
        for d, part in enumerate(shifted(value, column)):
            at = (x * 3 + d) * height
            cols_ref[at : at + height] = part.astype(BF16)

    column1 = lax.broadcasted_iota(jnp.int32, (w1_ref.shape[0], n), 1)
    w1 = w1_ref[:, : 9 * height]
    for x in range(ext - 2):
        at = x * 3 * height
        value = jnp.maximum(dot(w1, cols_ref[at : at + 9 * height]), 0.0)
        if x < rows - 1:
            value = value * x_low
        if x >= 2 * rows - 1:
            value = value * x_high
        value = jnp.concatenate(
            [value[: 2 * hid] * z_low, value[2 * hid : -2 * hid], value[-2 * hid :] * z_high], axis=0
        )
        for d, part in enumerate(shifted(value, column1)):
            a1_ref[x, d] = part.astype(BF16)

    blocks = 3
    out2 = 6 * hid
    for k in range(blocks):
        parts = {}
        for x in range(ext - 2):
            first = 0 if x <= ext - 5 else x - (ext - 5)
            last = min(x, 2)
            cols = jnp.concatenate([a1_ref[x, d, k * out2 : k * out2 + 256] for d in range(3)], axis=0)
            value = dot(w2_ref[first * out2 : (last + 1) * out2], cols)
            for dx in range(first, last + 1):
                piece = value[(dx - first) * out2 : (dx - first + 1) * out2]
                at = x - dx
                parts[at] = piece if at not in parts else parts[at] + piece
            done = x - 2
            if done >= 0:
                value = jnp.maximum(parts.pop(done), 0.0)
                if done < rows - 2:
                    value = value * x_low
                if done >= 2 * rows - 2:
                    value = value * x_high
                if k == 0:
                    value = jnp.concatenate([value[:hid] * z_low, value[hid:]], axis=0)
                if k == blocks - 1:
                    value = jnp.concatenate([value[:-hid], value[-hid:] * z_high], axis=0)
                a2_ref[done, k * out2 : (k + 1) * out2] = value.astype(BF16)

    depth = 16
    size = 2 * depth
    w3 = w3_ref[:, :576]
    terms = [dot(w3, a2_ref[x]) for x in range(rows + 2)]
    column3 = lax.broadcasted_iota(jnp.int32, (size, n), 1)
    for x in range(rows):
        sums = []
        for d in range(3):
            at = lambda dx: (dx * 3 + d) * size
            sums.append(sum(terms[x + dx][at(dx) : at(dx) + size] for dx in range(3)))
        value = sums[1] + jnp.where(column3 == 0, 0.0, pltpu.roll(sums[0], 1, 1))
        value = value + jnp.where(column3 == n - 1, 0.0, pltpu.roll(sums[2], n - 1, 1))
        half = own_ref[x].astype(F32)
        for p in range(2):
            mine = half[p * WIN + 4 : p * WIN + 4 + depth]
            out_ref[x, p] = mine + value[p * depth : (p + 1) * depth]


def regularized(place, low, own, high, w1, w2, w3, depth):
    rows, height, n = own.shape
    ext = 3 * rows
    return pl.pallas_call(
        conv_kernel,
        in_specs=[SMEM] + [VMEM] * 6,
        out_specs=VMEM,
        out_shape=jax.ShapeDtypeStruct((rows, 2, depth, n), F32),
        scratch_shapes=[
            pltpu.VMEM((ext * 3 * height, n), BF16),
            pltpu.VMEM((ext - 2, 3, 640, n), BF16),
            pltpu.VMEM((ext - 4, 576, n), BF16),
        ],
        compiler_params=pltpu.CompilerParams(vmem_limit_bytes=40 << 20),
        cost_estimate=pl.CostEstimate(flops=6 << 30, bytes_accessed=4 << 20, transcendentals=0),
        name="regularized",
    )(place, low, own, high, w1, w2, w3)


def weights_kernel(b1_ref, b2_ref, b3_ref, w1_ref, w2_ref, w3_ref):
    base = b1_ref[...].astype(F32)
    for a in range(20):
        moved = base if a == 0 else pltpu.roll(base, a, 1)
        w1_ref[a * 32 : (a + 1) * 32] = moved.astype(BF16)
    for dx in range(3):
        for dy in range(3):
            base = b2_ref[dx * 3 + dy].astype(F32)
            for a in range(6):
                moved = base if a == 0 else pltpu.roll(base, a * 32, 1)
                at = (dx * 6 + a) * 32
                w2_ref[at : at + 32, dy * 256 : (dy + 1) * 256] = moved.astype(BF16)
    base = b3_ref[...].astype(F32)
    for t in range(18):
        row = jnp.broadcast_to(base[t : t + 1], (16, base.shape[1]))
        moved = pltpu.roll(row, 0, 1, stride=16, stride_axis=0)
        moved = pltpu.roll(moved, 0, 1, stride=16, stride_axis=0)
        w3_ref[t * 16 : (t + 1) * 16] = moved.astype(BF16)


def banded_weights(conv_in, conv_mid, conv_out):
    b1 = jnp.pad(conv_in.transpose(0, 2, 4, 1, 3), ((0, 0),) * 4 + ((1, WIN - 4),))
    b1 = jnp.pad(b1.reshape(32, 18 * WIN), ((0, 0), (0, 512 - 18 * WIN)))
    b2 = conv_mid.transpose(2, 4, 0, 3, 1).reshape(9, 32, 96)
    b2 = jnp.pad(b2, ((0, 0), (0, 0), (0, 160)))
    b3 = conv_out.transpose(2, 4, 0, 3, 1).reshape(18, 96)
    b3 = jnp.pad(b3, ((0, 0), (0, 640 - 96)))
    return pl.pallas_call(
        weights_kernel,
        in_specs=[VMEM] * 3,
        out_specs=[VMEM] * 3,
        out_shape=[
            jax.ShapeDtypeStruct((640, 512), BF16),
            jax.ShapeDtypeStruct((576, 768), BF16),
            jax.ShapeDtypeStruct((288, 640), BF16),
        ],
        compiler_params=pltpu.CompilerParams(vmem_limit_bytes=16 << 20),
        name="banded_weights",
    )(b1, b2, b3)


def gathered(brick, chips):
    held = brick[None]
    for k in (4, 2, 1):
        came = lax.ppermute(held, "coil", [(i, i ^ (2 * k)) for i in range(2 * chips)])
        held = jnp.stack([held, came], axis=1).reshape(-1, *brick.shape)
    return held


def step(image, sensitivity, kspace, sampling, conv_in, conv_mid, conv_out):
    rows, parts, depth, n = image.shape
    coils, slabs = (lax.axis_size("coil"), lax.axis_size("slab"))
    coil, slab = (lax.axis_index("coil"), lax.axis_index("slab"))
    place = jnp.stack([coil, slab, plane_of(coil, slab)]).astype(jnp.int32)
    pairs = coils // 2
    chips = [[2 * i + c for i in range(pairs)] for c in range(2)]
    partner = [(i, i ^ 1) for i in range(coils)]
    there = [(a, b, coil_of(b, a)) for a in range(coils) for b in range(slabs)]
    across = [(a * slabs + b, c * slabs + a) for a, b, c in there]
    w1, w2, w3 = banded_weights(conv_in, conv_mid, conv_out)

    brick = lax.ppermute(image.astype(BF16), ("coil", "slab"), across)
    sens = lax.all_to_all(
        sensitivity[0].reshape(slabs, rows, parts, depth, n), "slab", 0, 0, tiled=True
    )
    img_a = gathered(brick, pairs)
    img_b = lax.ppermute(img_a, "coil", partner)

    kept, sent = coil_terms(place, sens, img_a, img_b, kspace[0], sampling, table(n))
    terms = pair_sum(kept, lax.ppermute(sent, "coil", partner))
    terms = lax.all_to_all(terms, "coil", 0, 0, tiled=True, axis_index_groups=chips)
    start = start_brick(place, terms, img_a, img_b)

    home = [(c * slabs + a, a * slabs + b) for a, b, c in there]
    up = [(i, i + 1) for i in range(coils - 1)]
    own = lax.ppermute(start, ("coil", "slab"), home)
    low = lax.ppermute(own, "coil", up)
    high = lax.ppermute(own, "coil", [(j, i) for i, j in up])
    return regularized(place, low, own, high, w1, w2, w3, depth)


def solution(mesh):
    return jax.shard_map(
        step,
        mesh=mesh,
        in_specs=(
            P("coil", None, "slab", None),
            P("coil", None, None, "slab", None),
            P("coil", "slab", None, None, None),
            P(),
            P(),
            P(),
            P(),
        ),
        out_specs=P("coil", None, "slab", None),
        check_vma=False,
    )
```

```python
import math

import jax
import jax.numpy as jnp
import numpy as np
from jax import lax
from jax.experimental import pallas as pl
from jax.experimental.pallas import tpu as pltpu
from jax.sharding import PartitionSpec as P

BF16 = jnp.bfloat16
F32 = jnp.float32
WIN = 24
VMEM = pl.BlockSpec(memory_space=pltpu.VMEM)
SMEM = pl.BlockSpec(memory_space=pltpu.SMEM)


def table(length):
    ramp = np.arange(length)
    angles = (ramp[:, None] * ramp[None, :] % length) * (2.0 * math.pi / length)
    re = np.cos(angles) / math.sqrt(length)
    im = -np.sin(angles) / math.sqrt(length)
    return jnp.asarray(np.concatenate([re, im, -im], axis=1), BF16)


def chip_of(z):
    return (z & 1) * 4 + (((z >> 1) + 2) & 3)


def plane_of(coil):
    chip = coil >> 1
    return (coil & 1) * 8 + (((chip - 2) & 3) << 1) + (chip >> 2)


def coil_of(plane):
    return 2 * chip_of(plane & 7) + (plane >> 3)


def dot(a, b):
    return jnp.dot(a, b, preferred_element_type=F32)


def coil_kernel(place_ref, sens_ref, img_a_ref, img_b_ref, ksp_ref, keep_ref, table_ref,
                keep_out, send_out, pad_ref):
    rows, n = (ksp_ref.shape[0], ksp_ref.shape[-1])
    half = img_a_ref.shape[0]
    coil = place_ref[0]
    chip, low_half = (coil >> 1, (coil & 1) == 0)
    at = [chip_of(z) for z in range(half)]

    def image_part(x, p):
        a = jnp.concatenate([img_a_ref[chip ^ at[z], x, p] for z in range(half)], axis=0)
        b = jnp.concatenate([img_b_ref[chip ^ at[z], x, p] for z in range(half)], axis=0)
        low, high = (jnp.where(low_half, a, b), jnp.where(low_half, b, a))
        return jnp.concatenate([low, high], axis=0).astype(F32)

    re, im, mi = (table_ref[:, i * n : (i + 1) * n] for i in range(3))
    fwd = jnp.concatenate([jnp.concatenate([re, im], axis=1), jnp.concatenate([mi, re], axis=1)], axis=0)
    bwd = jnp.concatenate([jnp.concatenate([re, mi], axis=1), jnp.concatenate([im, re], axis=1)], axis=0)
    keep = keep_ref[...].astype(F32)
    keep = jnp.concatenate([keep, keep], axis=0)
    edge = jnp.zeros((8, n), F32)
    depth = n // (2 * half)
    for x in range(rows):
        sr = sens_ref[:, x, 0].reshape(n, n).astype(F32)
        si = sens_ref[:, x, 1].reshape(n, n).astype(F32)
        mr, mi = (image_part(x, 0), image_part(x, 1))
        coil_image = jnp.concatenate([sr * mr - si * mi, sr * mi + si * mr], axis=1).astype(BF16)
        lines = dot(coil_image, fwd).astype(BF16)
        lines = jnp.concatenate([lines[:, :n], lines[:, n:]], axis=0)
        spectrum = dot(bwd, lines)
        misfit = (keep * (spectrum - ksp_ref[x].reshape(2 * n, n).astype(F32))).astype(BF16)
        back = dot(fwd, misfit).astype(BF16)
        back = jnp.concatenate([back[:n], back[n:]], axis=1)
        field = dot(back, bwd)
        fr, fi = (field[:, :n], field[:, n:])
        sr = sens_ref[:, x, 0].reshape(n, n).astype(F32)
        si = sens_ref[:, x, 1].reshape(n, n).astype(F32)
        for p in range(2):
            pad_ref[x, p, 0:8] = edge
            pad_ref[x, p, n + 8 : n + 16] = edge
        pad_ref[x, 0, 8 : n + 8] = sr * fr + si * fi
        pad_ref[x, 1, 8 : n + 8] = sr * fi - si * fr

        def window(j):
            first = j * depth + 4
            parts = [pad_ref[x, p, first : first + WIN] for p in range(2)]
            return jnp.concatenate(parts, axis=0).astype(BF16)

        for z in range(half):
            low, high = (window(z), window(half + z))
            keep_out[at[z], x] = jnp.where(low_half, low, high)
            send_out[at[z], x] = jnp.where(low_half, high, low)


def coil_terms(place, sens, img_a, img_b, ksp, keep, table):
    _, rows, _, _, n = sens.shape
    out = jax.ShapeDtypeStruct((img_a.shape[0], rows, 2 * WIN, n), BF16)
    return pl.pallas_call(
        coil_kernel,
        in_specs=[SMEM] + [VMEM] * 6,
        out_specs=[VMEM, VMEM],
        out_shape=[out, out],
        scratch_shapes=[pltpu.VMEM((rows, 2, n + 16, n), F32)],
        compiler_params=pltpu.CompilerParams(vmem_limit_bytes=40 << 20),
        cost_estimate=pl.CostEstimate(
            flops=rows * 16 * 2 * n * n * n, bytes_accessed=6 << 20, transcendentals=0
        ),
        name="coil_terms",
    )(place, sens, img_a, img_b, ksp, keep, table)


def pair_kernel(a_ref, b_ref, out_ref):
    out_ref[...] = a_ref[...] + b_ref[...]


def pair_sum(a, b):
    return pl.pallas_call(
        pair_kernel,
        in_specs=[VMEM, VMEM],
        out_specs=VMEM,
        out_shape=jax.ShapeDtypeStruct(a.shape, a.dtype),
        compiler_params=pltpu.CompilerParams(vmem_limit_bytes=16 << 20),
        name="pair_sum",
    )(a, b)


def start_kernel(place_ref, terms_ref, img_a_ref, img_b_ref, out_ref, grad_ref):
    pairs, rows = (terms_ref.shape[0], terms_ref.shape[1])
    coil, plane = (place_ref[0], place_ref[2])
    chip, half = (coil >> 1, coil & 1)
    below, above = (jnp.maximum(plane - 1, 0), jnp.minimum(plane + 1, 2 * pairs - 1))
    low_ok = jnp.where(plane > 0, 1.0, 0.0).astype(F32)
    high_ok = jnp.where(plane < 2 * pairs - 1, 1.0, 0.0).astype(F32)

    def brick(j, x, p):
        slot = chip ^ chip_of(j & 7)
        value = jnp.where((j >> 3) == half, img_a_ref[slot, x, p], img_b_ref[slot, x, p])
        return value.astype(F32)

    depth = img_a_ref.shape[3]
    for x in range(rows):
        total = terms_ref[0, x].astype(F32)
        for k in range(1, pairs):
            total += terms_ref[k, x].astype(F32)
        pieces = []
        for p in range(2):
            low = brick(below, x, p)[depth - 8 :] * low_ok
            own = img_a_ref[0, x, p].astype(F32)
            high = brick(above, x, p)[:8] * high_ok
            pieces.append(jnp.concatenate([low, own, high], axis=0)[4 : 4 + WIN])
        out_ref[x] = (jnp.concatenate(pieces, axis=0) - total).astype(BF16)
        for p in range(2):
            grad_ref[x, p] = total[p * WIN + 4 : p * WIN + 4 + depth]


def start_brick(place, terms, img_a, img_b):
    _, rows, height, n = terms.shape
    return pl.pallas_call(
        start_kernel,
        in_specs=[SMEM, VMEM, VMEM, VMEM],
        out_specs=[VMEM, VMEM],
        out_shape=[
            jax.ShapeDtypeStruct((rows, height, n), BF16),
            jax.ShapeDtypeStruct((rows, *img_a.shape[2:]), F32),
        ],
        compiler_params=pltpu.CompilerParams(vmem_limit_bytes=16 << 20),
        name="start_brick",
    )(place, terms, img_a, img_b)


def shifted(value, column):
    n = value.shape[1]
    before = jnp.where(column == 0, 0.0, pltpu.roll(value, 1, 1))
    after = jnp.where(column == n - 1, 0.0, pltpu.roll(value, n - 1, 1))
    return before, value, after


def conv_kernel(place_ref, low_ref, own_ref, high_ref, grad_ref, w1_ref, w2_ref, w3_ref, out_ref,
                cols_ref, a1_ref, a2_ref):
    rows, height, n = own_ref.shape
    hid = 32
    ext = 3 * rows
    brick, plane = (place_ref[1], place_ref[2])
    flag = lambda ok: jnp.where(ok, 1.0, 0.0).astype(F32)
    x_low, x_high = (flag(brick > 0), flag(brick < 48 // rows - 1))
    z_low, z_high = (flag(plane > 0), flag(plane < 256 // 16 - 1))

    for x in range(ext):
        src = (low_ref, own_ref, high_ref)[x // rows]
        value = src[x % rows].astype(F32)
        column = lax.broadcasted_iota(jnp.int32, value.shape, 1)
        for d, part in enumerate(shifted(value, column)):
            at = (x * 3 + d) * height
            cols_ref[at : at + height] = part.astype(BF16)

    column1 = lax.broadcasted_iota(jnp.int32, (w1_ref.shape[0], n), 1)
    w1 = w1_ref[:, : 9 * height]
    for x in range(ext - 2):
        at = x * 3 * height
        value = jnp.maximum(dot(w1, cols_ref[at : at + 9 * height]), 0.0)
        if x < rows - 1:
            value = value * x_low
        if x >= 2 * rows - 1:
            value = value * x_high
        value = jnp.concatenate(
            [value[: 2 * hid] * z_low, value[2 * hid : -2 * hid], value[-2 * hid :] * z_high], axis=0
        )
        for d, part in enumerate(shifted(value, column1)):
            a1_ref[x, d] = part.astype(BF16)

    blocks = 3
    out2 = 6 * hid
    for k in range(blocks):
        parts = {}
        for x in range(ext - 2):
            first = 0 if x <= ext - 5 else x - (ext - 5)
            last = min(x, 2)
            cols = jnp.concatenate([a1_ref[x, d, k * out2 : k * out2 + 256] for d in range(3)], axis=0)
            value = dot(w2_ref[first * out2 : (last + 1) * out2], cols)
            for dx in range(first, last + 1):
                piece = value[(dx - first) * out2 : (dx - first + 1) * out2]
                at = x - dx
                parts[at] = piece if at not in parts else parts[at] + piece
            done = x - 2
            if done >= 0:
                value = jnp.maximum(parts.pop(done), 0.0)
                if done < rows - 2:
                    value = value * x_low
                if done >= 2 * rows - 2:
                    value = value * x_high
                if k == 0:
                    value = jnp.concatenate([value[:hid] * z_low, value[hid:]], axis=0)
                if k == blocks - 1:
                    value = jnp.concatenate([value[:-hid], value[-hid:] * z_high], axis=0)
                a2_ref[done, k * out2 : (k + 1) * out2] = value.astype(BF16)

    depth = 16
    size = 2 * depth
    w3 = w3_ref[:, :576]
    terms = [dot(w3, a2_ref[x]) for x in range(rows + 2)]
    column3 = lax.broadcasted_iota(jnp.int32, (size, n), 1)
    for x in range(rows):
        sums = []
        for d in range(3):
            at = lambda dx: (dx * 3 + d) * size
            sums.append(sum(terms[x + dx][at(dx) : at(dx) + size] for dx in range(3)))
        value = sums[1] + jnp.where(column3 == 0, 0.0, pltpu.roll(sums[0], 1, 1))
        value = value + jnp.where(column3 == n - 1, 0.0, pltpu.roll(sums[2], n - 1, 1))
        for p in range(2):
            out_ref[x, p] = (value[p * depth : (p + 1) * depth] - grad_ref[x, p]).astype(BF16)


def regularized(place, low, own, high, grad, w1, w2, w3):
    rows, height, n = own.shape
    ext = 3 * rows
    return pl.pallas_call(
        conv_kernel,
        in_specs=[SMEM] + [VMEM] * 7,
        out_specs=VMEM,
        out_shape=jax.ShapeDtypeStruct(grad.shape, BF16),
        scratch_shapes=[
            pltpu.VMEM((ext * 3 * height, n), BF16),
            pltpu.VMEM((ext - 2, 3, 640, n), BF16),
            pltpu.VMEM((ext - 4, 576, n), BF16),
        ],
        compiler_params=pltpu.CompilerParams(vmem_limit_bytes=40 << 20),
        cost_estimate=pl.CostEstimate(flops=6 << 30, bytes_accessed=4 << 20, transcendentals=0),
        name="regularized",
    )(place, low, own, high, grad, w1, w2, w3)


def weights_kernel(b1_ref, b2_ref, b3_ref, w1_ref, w2_ref, w3_ref):
    base = b1_ref[...].astype(F32)
    for a in range(20):
        moved = base if a == 0 else pltpu.roll(base, a, 1)
        w1_ref[a * 32 : (a + 1) * 32] = moved.astype(BF16)
    for dx in range(3):
        for dy in range(3):
            base = b2_ref[dx * 3 + dy].astype(F32)
            for a in range(6):
                moved = base if a == 0 else pltpu.roll(base, a * 32, 1)
                at = (dx * 6 + a) * 32
                w2_ref[at : at + 32, dy * 256 : (dy + 1) * 256] = moved.astype(BF16)
    base = b3_ref[...].astype(F32)
    for t in range(18):
        row = jnp.broadcast_to(base[t : t + 1], (16, base.shape[1]))
        moved = pltpu.roll(row, 0, 1, stride=16, stride_axis=0)
        moved = pltpu.roll(moved, 0, 1, stride=16, stride_axis=0)
        w3_ref[t * 16 : (t + 1) * 16] = moved.astype(BF16)


def banded_weights(conv_in, conv_mid, conv_out):
    b1 = jnp.pad(conv_in.transpose(0, 2, 4, 1, 3), ((0, 0),) * 4 + ((1, WIN - 4),))
    b1 = jnp.pad(b1.reshape(32, 18 * WIN), ((0, 0), (0, 512 - 18 * WIN)))
    b2 = conv_mid.transpose(2, 4, 0, 3, 1).reshape(9, 32, 96)
    b2 = jnp.pad(b2, ((0, 0), (0, 0), (0, 160)))
    b3 = conv_out.transpose(2, 4, 0, 3, 1).reshape(18, 96)
    b3 = jnp.pad(b3, ((0, 0), (0, 640 - 96)))
    return pl.pallas_call(
        weights_kernel,
        in_specs=[VMEM] * 3,
        out_specs=[VMEM] * 3,
        out_shape=[
            jax.ShapeDtypeStruct((640, 512), BF16),
            jax.ShapeDtypeStruct((576, 768), BF16),
            jax.ShapeDtypeStruct((288, 640), BF16),
        ],
        compiler_params=pltpu.CompilerParams(vmem_limit_bytes=16 << 20),
        name="banded_weights",
    )(b1, b2, b3)


def gathered(brick, chips):
    hop = lambda v, k: lax.ppermute(v, "coil", [(i, i ^ (2 * k)) for i in range(2 * chips)])
    held = jnp.stack([brick] + [hop(brick, k) for k in (2, 4, 6)])
    return jnp.stack([held, hop(held, 1)], axis=1).reshape(-1, *brick.shape)


def step(image, sensitivity, kspace, sampling, conv_in, conv_mid, conv_out):
    rows, parts, depth, n = image.shape
    coils, slabs = (lax.axis_size("coil"), lax.axis_size("slab"))
    coil, slab = (lax.axis_index("coil"), lax.axis_index("slab"))
    place = jnp.stack([coil, slab, plane_of(coil)]).astype(jnp.int32)
    pairs = coils // 2
    chips = [[2 * i + c for i in range(pairs)] for c in range(2)]
    partner = [(i, i ^ 1) for i in range(coils)]
    there = [(a, b, coil_of(b)) for a in range(coils) for b in range(slabs)]
    across = [(a * slabs + b, c * slabs + a) for a, b, c in there]
    w1, w2, w3 = banded_weights(conv_in, conv_mid, conv_out)

    brick = lax.ppermute(image.astype(BF16), ("coil", "slab"), across)
    sens = lax.all_to_all(
        sensitivity[0].reshape(slabs, rows, parts, depth, n), "slab", 0, 0, tiled=True
    )
    img_a = gathered(brick, pairs)
    img_b = lax.ppermute(img_a, "coil", partner)

    kept, sent = coil_terms(place, sens, img_a, img_b, kspace[0], sampling, table(n))
    terms = pair_sum(kept, lax.ppermute(sent, "coil", partner))
    terms = lax.all_to_all(terms, "coil", 0, 0, tiled=True, axis_index_groups=chips)
    start, grad = start_brick(place, terms, img_a, img_b)

    up = [(i, i + 1) for i in range(slabs - 1)]
    low = lax.ppermute(start, "slab", up)
    high = lax.ppermute(start, "slab", [(j, i) for i, j in up])
    change = regularized(place, low, start, high, grad, w1, w2, w3)
    change = lax.ppermute(
        change, ("coil", "slab"), [(c * slabs + a, a * slabs + b) for a, b, c in there]
    )
    return image + change.astype(F32)


def solution(mesh):
    return jax.shard_map(
        step,
        mesh=mesh,
        in_specs=(
            P("coil", None, "slab", None),
            P("coil", None, None, "slab", None),
            P("coil", "slab", None, None, None),
            P(),
            P(),
            P(),
            P(),
        ),
        out_specs=P("coil", None, "slab", None),
        check_vma=False,
    )
```

```python
import math

import jax
import jax.numpy as jnp
import numpy as np
from jax import lax
from jax.experimental import pallas as pl
from jax.experimental.pallas import tpu as pltpu
from jax.sharding import PartitionSpec as P

BF16 = jnp.bfloat16
F32 = jnp.float32
WIN = 24
VMEM = pl.BlockSpec(memory_space=pltpu.VMEM)
SMEM = pl.BlockSpec(memory_space=pltpu.SMEM)


def table(length):
    ramp = np.arange(length)
    angles = (ramp[:, None] * ramp[None, :] % length) * (2.0 * math.pi / length)
    re = np.cos(angles) / math.sqrt(length)
    im = -np.sin(angles) / math.sqrt(length)
    return jnp.asarray(np.concatenate([re, im, -im], axis=1), BF16)


def chip_of(z):
    return (z & 1) * 4 + (((z >> 1) + 2) & 3)


def plane_of(coil):
    chip = coil >> 1
    return (coil & 1) * 8 + (((chip - 2) & 3) << 1) + (chip >> 2)


def coil_of(plane):
    return 2 * chip_of(plane & 7) + (plane >> 3)


def dot(a, b):
    return jnp.dot(a, b, preferred_element_type=F32)


def coil_kernel(place_ref, sens_ref, img_a_ref, img_b_ref, ksp_ref, keep_ref, table_ref,
                keep_out, send_out, pad_ref):
    rows, n = (ksp_ref.shape[0], ksp_ref.shape[-1])
    half = img_a_ref.shape[0]
    coil = place_ref[0]
    chip, low_half = (coil >> 1, (coil & 1) == 0)
    at = [chip_of(z) for z in range(half)]

    def image_part(x, p):
        a = jnp.concatenate([img_a_ref[chip ^ at[z], x, p] for z in range(half)], axis=0)
        b = jnp.concatenate([img_b_ref[chip ^ at[z], x, p] for z in range(half)], axis=0)
        low, high = (jnp.where(low_half, a, b), jnp.where(low_half, b, a))
        return jnp.concatenate([low, high], axis=0).astype(F32)

    re, im, mi = (table_ref[:, i * n : (i + 1) * n] for i in range(3))
    fwd = jnp.concatenate([jnp.concatenate([re, im], axis=1), jnp.concatenate([mi, re], axis=1)], axis=0)
    bwd = jnp.concatenate([jnp.concatenate([re, mi], axis=1), jnp.concatenate([im, re], axis=1)], axis=0)
    keep = keep_ref[...].astype(F32)
    keep = jnp.concatenate([keep, keep], axis=0)
    edge = jnp.zeros((8, n), F32)
    depth = n // (2 * half)
    lines, misfits, fields = ([], [], [])
    for x in range(rows):
        sr = sens_ref[:, x, 0].reshape(n, n).astype(F32)
        si = sens_ref[:, x, 1].reshape(n, n).astype(F32)
        mr, mi = (image_part(x, 0), image_part(x, 1))
        coil_image = jnp.concatenate([sr * mr - si * mi, sr * mi + si * mr], axis=1).astype(BF16)
        lines.append(dot(coil_image, fwd).astype(BF16))
    for x in range(rows):
        line = jnp.concatenate([lines[x][:, :n], lines[x][:, n:]], axis=0)
        spectrum = dot(bwd, line)
        misfits.append((keep * (spectrum - ksp_ref[x].reshape(2 * n, n).astype(F32))).astype(BF16))
    for x in range(rows):
        back = dot(fwd, misfits[x]).astype(BF16)
        fields.append(jnp.concatenate([back[:n], back[n:]], axis=1))
    for x in range(rows):
        field = dot(fields[x], bwd)
        fr, fi = (field[:, :n], field[:, n:])
        sr = sens_ref[:, x, 0].reshape(n, n).astype(F32)
        si = sens_ref[:, x, 1].reshape(n, n).astype(F32)
        for p in range(2):
            pad_ref[x, p, 0:8] = edge
            pad_ref[x, p, n + 8 : n + 16] = edge
        pad_ref[x, 0, 8 : n + 8] = sr * fr + si * fi
        pad_ref[x, 1, 8 : n + 8] = sr * fi - si * fr

        def window(j):
            first = j * depth + 4
            parts = [pad_ref[x, p, first : first + WIN] for p in range(2)]
            return jnp.concatenate(parts, axis=0).astype(BF16)

        for z in range(half):
            low, high = (window(z), window(half + z))
            keep_out[at[z], x] = jnp.where(low_half, low, high)
            send_out[at[z], x] = jnp.where(low_half, high, low)


def coil_terms(place, sens, img_a, img_b, ksp, keep, table):
    _, rows, _, _, n = sens.shape
    out = jax.ShapeDtypeStruct((img_a.shape[0], rows, 2 * WIN, n), BF16)
    return pl.pallas_call(
        coil_kernel,
        in_specs=[SMEM] + [VMEM] * 6,
        out_specs=[VMEM, VMEM],
        out_shape=[out, out],
        scratch_shapes=[pltpu.VMEM((rows, 2, n + 16, n), F32)],
        compiler_params=pltpu.CompilerParams(vmem_limit_bytes=40 << 20),
        cost_estimate=pl.CostEstimate(
            flops=rows * 16 * 2 * n * n * n, bytes_accessed=6 << 20, transcendentals=0
        ),
        name="coil_terms",
    )(place, sens, img_a, img_b, ksp, keep, table)


def pair_kernel(a_ref, b_ref, out_ref):
    out_ref[...] = a_ref[...] + b_ref[...]


def pair_sum(a, b):
    return pl.pallas_call(
        pair_kernel,
        in_specs=[VMEM, VMEM],
        out_specs=VMEM,
        out_shape=jax.ShapeDtypeStruct(a.shape, a.dtype),
        compiler_params=pltpu.CompilerParams(vmem_limit_bytes=16 << 20),
        name="pair_sum",
    )(a, b)


def start_kernel(place_ref, terms_ref, img_a_ref, img_b_ref, out_ref, grad_ref):
    pairs, rows = (terms_ref.shape[0], terms_ref.shape[1])
    coil, plane = (place_ref[0], place_ref[2])
    chip, half = (coil >> 1, coil & 1)
    below, above = (jnp.maximum(plane - 1, 0), jnp.minimum(plane + 1, 2 * pairs - 1))
    low_ok = jnp.where(plane > 0, 1.0, 0.0).astype(F32)
    high_ok = jnp.where(plane < 2 * pairs - 1, 1.0, 0.0).astype(F32)

    def brick(j, x, p):
        slot = chip ^ chip_of(j & 7)
        value = jnp.where((j >> 3) == half, img_a_ref[slot, x, p], img_b_ref[slot, x, p])
        return value.astype(F32)

    depth = img_a_ref.shape[3]
    for x in range(rows):
        total = terms_ref[0, x].astype(F32)
        for k in range(1, pairs):
            total += terms_ref[k, x].astype(F32)
        pieces = []
        for p in range(2):
            low = brick(below, x, p)[depth - 8 :] * low_ok
            own = img_a_ref[0, x, p].astype(F32)
            high = brick(above, x, p)[:8] * high_ok
            pieces.append(jnp.concatenate([low, own, high], axis=0)[4 : 4 + WIN])
        out_ref[x] = (jnp.concatenate(pieces, axis=0) - total).astype(BF16)
        for p in range(2):
            grad_ref[x, p] = total[p * WIN + 4 : p * WIN + 4 + depth]


def start_brick(place, terms, img_a, img_b):
    _, rows, height, n = terms.shape
    return pl.pallas_call(
        start_kernel,
        in_specs=[SMEM, VMEM, VMEM, VMEM],
        out_specs=[VMEM, VMEM],
        out_shape=[
            jax.ShapeDtypeStruct((rows, height, n), BF16),
            jax.ShapeDtypeStruct((rows, *img_a.shape[2:]), F32),
        ],
        compiler_params=pltpu.CompilerParams(vmem_limit_bytes=16 << 20),
        name="start_brick",
    )(place, terms, img_a, img_b)


def shifted(value, column):
    n = value.shape[1]
    before = jnp.where(column == 0, 0.0, pltpu.roll(value, 1, 1))
    after = jnp.where(column == n - 1, 0.0, pltpu.roll(value, n - 1, 1))
    return before, value, after


def conv_kernel(place_ref, low_ref, own_ref, high_ref, grad_ref, w1_ref, w2_ref, w3_ref, out_ref,
                cols_ref, a1_ref, a2_ref):
    rows, height, n = own_ref.shape
    hid = 32
    ext = 3 * rows
    brick, plane = (place_ref[1], place_ref[2])
    flag = lambda ok: jnp.where(ok, 1.0, 0.0).astype(F32)
    x_low, x_high = (flag(brick > 0), flag(brick < 48 // rows - 1))
    z_low, z_high = (flag(plane > 0), flag(plane < 256 // 16 - 1))

    for x in range(ext):
        src = (low_ref, own_ref, high_ref)[x // rows]
        value = src[x % rows].astype(F32)
        column = lax.broadcasted_iota(jnp.int32, value.shape, 1)
        for d, part in enumerate(shifted(value, column)):
            at = (x * 3 + d) * height
            cols_ref[at : at + height] = part.astype(BF16)

    column1 = lax.broadcasted_iota(jnp.int32, (w1_ref.shape[0], n), 1)
    w1 = w1_ref[:, : 9 * height]
    for x in range(ext - 2):
        at = x * 3 * height
        value = jnp.maximum(dot(w1, cols_ref[at : at + 9 * height]), 0.0)
        if x < rows - 1:
            value = value * x_low
        if x >= 2 * rows - 1:
            value = value * x_high
        value = jnp.concatenate(
            [value[: 2 * hid] * z_low, value[2 * hid : -2 * hid], value[-2 * hid :] * z_high], axis=0
        )
        for d, part in enumerate(shifted(value, column1)):
            a1_ref[x, d] = part.astype(BF16)

    blocks = 3
    out2 = 6 * hid
    for k in range(blocks):
        parts = {}
        for x in range(ext - 2):
            first = 0 if x <= ext - 5 else x - (ext - 5)
            last = min(x, 2)
            cols = jnp.concatenate([a1_ref[x, d, k * out2 : k * out2 + 256] for d in range(3)], axis=0)
            value = dot(w2_ref[first * out2 : (last + 1) * out2], cols)
            for dx in range(first, last + 1):
                piece = value[(dx - first) * out2 : (dx - first + 1) * out2]
                at = x - dx
                parts[at] = piece if at not in parts else parts[at] + piece
            done = x - 2
            if done >= 0:
                value = jnp.maximum(parts.pop(done), 0.0)
                if done < rows - 2:
                    value = value * x_low
                if done >= 2 * rows - 2:
                    value = value * x_high
                if k == 0:
                    value = jnp.concatenate([value[:hid] * z_low, value[hid:]], axis=0)
                if k == blocks - 1:
                    value = jnp.concatenate([value[:-hid], value[-hid:] * z_high], axis=0)
                a2_ref[done, k * out2 : (k + 1) * out2] = value.astype(BF16)

    depth = 16
    size = 2 * depth
    w3 = w3_ref[:, :576]
    terms = [dot(w3, a2_ref[x]) for x in range(rows + 2)]
    column3 = lax.broadcasted_iota(jnp.int32, (size, n), 1)
    for x in range(rows):
        sums = []
        for d in range(3):
            at = lambda dx: (dx * 3 + d) * size
            sums.append(sum(terms[x + dx][at(dx) : at(dx) + size] for dx in range(3)))
        value = sums[1] + jnp.where(column3 == 0, 0.0, pltpu.roll(sums[0], 1, 1))
        value = value + jnp.where(column3 == n - 1, 0.0, pltpu.roll(sums[2], n - 1, 1))
        for p in range(2):
            out_ref[x, p] = (value[p * depth : (p + 1) * depth] - grad_ref[x, p]).astype(BF16)


def regularized(place, low, own, high, grad, w1, w2, w3):
    rows, height, n = own.shape
    ext = 3 * rows
    return pl.pallas_call(
        conv_kernel,
        in_specs=[SMEM] + [VMEM] * 7,
        out_specs=VMEM,
        out_shape=jax.ShapeDtypeStruct(grad.shape, BF16),
        scratch_shapes=[
            pltpu.VMEM((ext * 3 * height, n), BF16),
            pltpu.VMEM((ext - 2, 3, 640, n), BF16),
            pltpu.VMEM((ext - 4, 576, n), BF16),
        ],
        compiler_params=pltpu.CompilerParams(vmem_limit_bytes=40 << 20),
        cost_estimate=pl.CostEstimate(flops=6 << 30, bytes_accessed=4 << 20, transcendentals=0),
        name="regularized",
    )(place, low, own, high, grad, w1, w2, w3)


def weights_kernel(b1_ref, b2_ref, b3_ref, w1_ref, w2_ref, w3_ref):
    base = b1_ref[...].astype(F32)
    for a in range(20):
        moved = base if a == 0 else pltpu.roll(base, a, 1)
        w1_ref[a * 32 : (a + 1) * 32] = moved.astype(BF16)
    for dx in range(3):
        for dy in range(3):
            base = b2_ref[dx * 3 + dy].astype(F32)
            for a in range(6):
                moved = base if a == 0 else pltpu.roll(base, a * 32, 1)
                at = (dx * 6 + a) * 32
                w2_ref[at : at + 32, dy * 256 : (dy + 1) * 256] = moved.astype(BF16)
    base = b3_ref[...].astype(F32)
    for t in range(18):
        row = jnp.broadcast_to(base[t : t + 1], (16, base.shape[1]))
        moved = pltpu.roll(row, 0, 1, stride=16, stride_axis=0)
        moved = pltpu.roll(moved, 0, 1, stride=16, stride_axis=0)
        w3_ref[t * 16 : (t + 1) * 16] = moved.astype(BF16)


def banded_weights(conv_in, conv_mid, conv_out):
    b1 = jnp.pad(conv_in.transpose(0, 2, 4, 1, 3), ((0, 0),) * 4 + ((1, WIN - 4),))
    b1 = jnp.pad(b1.reshape(32, 18 * WIN), ((0, 0), (0, 512 - 18 * WIN)))
    b2 = conv_mid.transpose(2, 4, 0, 3, 1).reshape(9, 32, 96)
    b2 = jnp.pad(b2, ((0, 0), (0, 0), (0, 160)))
    b3 = conv_out.transpose(2, 4, 0, 3, 1).reshape(18, 96)
    b3 = jnp.pad(b3, ((0, 0), (0, 640 - 96)))
    return pl.pallas_call(
        weights_kernel,
        in_specs=[VMEM] * 3,
        out_specs=[VMEM] * 3,
        out_shape=[
            jax.ShapeDtypeStruct((640, 512), BF16),
            jax.ShapeDtypeStruct((576, 768), BF16),
            jax.ShapeDtypeStruct((288, 640), BF16),
        ],
        compiler_params=pltpu.CompilerParams(vmem_limit_bytes=16 << 20),
        name="banded_weights",
    )(b1, b2, b3)


def gathered(brick, chips):
    hop = lambda v, k: lax.ppermute(v, "coil", [(i, i ^ (2 * k)) for i in range(2 * chips)])
    held = jnp.stack([brick] + [hop(brick, k) for k in (2, 4, 6)])
    return jnp.stack([held, hop(held, 1)], axis=1).reshape(-1, *brick.shape)


def step(image, sensitivity, kspace, sampling, conv_in, conv_mid, conv_out):
    rows, parts, depth, n = image.shape
    coils, slabs = (lax.axis_size("coil"), lax.axis_size("slab"))
    coil, slab = (lax.axis_index("coil"), lax.axis_index("slab"))
    place = jnp.stack([coil, slab, plane_of(coil)]).astype(jnp.int32)
    pairs = coils // 2
    chips = [[2 * i + c for i in range(pairs)] for c in range(2)]
    partner = [(i, i ^ 1) for i in range(coils)]
    there = [(a, b, coil_of(b)) for a in range(coils) for b in range(slabs)]
    across = [(a * slabs + b, c * slabs + a) for a, b, c in there]
    w1, w2, w3 = banded_weights(conv_in, conv_mid, conv_out)

    brick = lax.ppermute(image.astype(BF16), ("coil", "slab"), across)
    sens = lax.all_to_all(
        sensitivity[0].reshape(slabs, rows, parts, depth, n), "slab", 0, 0, tiled=True
    )
    img_a = gathered(brick, pairs)
    img_b = lax.ppermute(img_a, "coil", partner)

    kept, sent = coil_terms(place, sens, img_a, img_b, kspace[0], sampling, table(n))
    terms = pair_sum(kept, lax.ppermute(sent, "coil", partner))
    terms = lax.all_to_all(terms, "coil", 0, 0, tiled=True, axis_index_groups=chips)
    start, grad = start_brick(place, terms, img_a, img_b)

    up = [(i, i + 1) for i in range(slabs - 1)]
    low = lax.ppermute(start, "slab", up)
    high = lax.ppermute(start, "slab", [(j, i) for i, j in up])
    change = regularized(place, low, start, high, grad, w1, w2, w3)
    change = lax.ppermute(
        change, ("coil", "slab"), [(c * slabs + a, a * slabs + b) for a, b, c in there]
    )
    return image + change.astype(F32)


def solution(mesh):
    return jax.shard_map(
        step,
        mesh=mesh,
        in_specs=(
            P("coil", None, "slab", None),
            P("coil", None, None, "slab", None),
            P("coil", "slab", None, None, None),
            P(),
            P(),
            P(),
            P(),
        ),
        out_specs=P("coil", None, "slab", None),
        check_vma=False,
    )
```

```python
import math

import jax
import jax.numpy as jnp
import numpy as np
from jax import lax
from jax.experimental import pallas as pl
from jax.experimental.pallas import tpu as pltpu
from jax.sharding import PartitionSpec as P

BF16 = jnp.bfloat16
F32 = jnp.float32
WIN = 24
VMEM = pl.BlockSpec(memory_space=pltpu.VMEM)
SMEM = pl.BlockSpec(memory_space=pltpu.SMEM)


def table(length):
    ramp = np.arange(length)
    angles = (ramp[:, None] * ramp[None, :] % length) * (2.0 * math.pi / length)
    re = np.cos(angles) / math.sqrt(length)
    im = -np.sin(angles) / math.sqrt(length)
    return jnp.asarray(np.concatenate([re, im, -im], axis=1), BF16)


def chip_of(z):
    return (z & 1) * 4 + (((z >> 1) + 2) & 3)


def plane_of(coil):
    chip = coil >> 1
    return (coil & 1) * 8 + (((chip - 2) & 3) << 1) + (chip >> 2)


def coil_of(plane):
    return 2 * chip_of(plane & 7) + (plane >> 3)


def dot(a, b):
    return jnp.dot(a, b, preferred_element_type=F32)


def coil_kernel(place_ref, sens_ref, img_a_ref, img_b_ref, ksp_ref, keep_ref, table_ref,
                keep_out, send_out, pad_ref):
    rows, n = (ksp_ref.shape[0], ksp_ref.shape[-1])
    half = img_a_ref.shape[0]
    coil = place_ref[0]
    chip, low_half = (coil >> 1, (coil & 1) == 0)
    at = [chip_of(z) for z in range(half)]

    def image_part(x, p):
        a = jnp.concatenate([img_a_ref[chip ^ at[z], x, p] for z in range(half)], axis=0)
        b = jnp.concatenate([img_b_ref[chip ^ at[z], x, p] for z in range(half)], axis=0)
        low, high = (jnp.where(low_half, a, b), jnp.where(low_half, b, a))
        return jnp.concatenate([low, high], axis=0).astype(F32)

    re, im, mi = (table_ref[:, i * n : (i + 1) * n] for i in range(3))
    fwd = jnp.concatenate([jnp.concatenate([re, im], axis=1), jnp.concatenate([mi, re], axis=1)], axis=0)
    bwd = jnp.concatenate([jnp.concatenate([re, mi], axis=1), jnp.concatenate([im, re], axis=1)], axis=0)
    keep = keep_ref[...].astype(F32)
    keep = jnp.concatenate([keep, keep], axis=0)
    edge = jnp.zeros((8, n), F32)
    depth = n // (2 * half)
    lines, misfits, fields = ([], [], [])
    for x in range(rows):
        sr = sens_ref[:, x, 0].reshape(n, n).astype(F32)
        si = sens_ref[:, x, 1].reshape(n, n).astype(F32)
        mr, mi = (image_part(x, 0), image_part(x, 1))
        coil_image = jnp.concatenate([sr * mr - si * mi, sr * mi + si * mr], axis=1).astype(BF16)
        lines.append(dot(coil_image, fwd).astype(BF16))
    for x in range(rows):
        line = jnp.concatenate([lines[x][:, :n], lines[x][:, n:]], axis=0)
        spectrum = dot(bwd, line)
        misfits.append((keep * (spectrum - ksp_ref[x].reshape(2 * n, n).astype(F32))).astype(BF16))
    for x in range(rows):
        back = dot(fwd, misfits[x]).astype(BF16)
        fields.append(jnp.concatenate([back[:n], back[n:]], axis=1))
    for x in range(rows):
        field = dot(fields[x], bwd)
        fr, fi = (field[:, :n], field[:, n:])
        sr = sens_ref[:, x, 0].reshape(n, n).astype(F32)
        si = sens_ref[:, x, 1].reshape(n, n).astype(F32)
        for p in range(2):
            pad_ref[x, p, 0:8] = edge
            pad_ref[x, p, n + 8 : n + 16] = edge
        pad_ref[x, 0, 8 : n + 8] = sr * fr + si * fi
        pad_ref[x, 1, 8 : n + 8] = sr * fi - si * fr

        def window(j):
            first = j * depth + 4
            parts = [pad_ref[x, p, first : first + WIN] for p in range(2)]
            return jnp.concatenate(parts, axis=0).astype(BF16)

        for z in range(half):
            low, high = (window(z), window(half + z))
            keep_out[at[z], x] = jnp.where(low_half, low, high)
            send_out[at[z], x] = jnp.where(low_half, high, low)


def coil_terms(place, sens, img_a, img_b, ksp, keep, table):
    _, rows, _, _, n = sens.shape
    out = jax.ShapeDtypeStruct((img_a.shape[0], rows, 2 * WIN, n), BF16)
    return pl.pallas_call(
        coil_kernel,
        in_specs=[SMEM] + [VMEM] * 6,
        out_specs=[VMEM, VMEM],
        out_shape=[out, out],
        scratch_shapes=[pltpu.VMEM((rows, 2, n + 16, n), F32)],
        compiler_params=pltpu.CompilerParams(vmem_limit_bytes=40 << 20),
        cost_estimate=pl.CostEstimate(
            flops=rows * 16 * 2 * n * n * n, bytes_accessed=6 << 20, transcendentals=0
        ),
        name="coil_terms",
    )(place, sens, img_a, img_b, ksp, keep, table)


def pair_kernel(a_ref, b_ref, out_ref):
    out_ref[...] = a_ref[...] + b_ref[...]


def pair_sum(a, b):
    return pl.pallas_call(
        pair_kernel,
        in_specs=[VMEM, VMEM],
        out_specs=VMEM,
        out_shape=jax.ShapeDtypeStruct(a.shape, a.dtype),
        compiler_params=pltpu.CompilerParams(vmem_limit_bytes=16 << 20),
        name="pair_sum",
    )(a, b)


def start_kernel(place_ref, terms_ref, img_a_ref, img_b_ref, out_ref, grad_ref):
    pairs, rows = (terms_ref.shape[0], terms_ref.shape[1])
    coil, plane = (place_ref[0], place_ref[2])
    chip, half = (coil >> 1, coil & 1)
    below, above = (jnp.maximum(plane - 1, 0), jnp.minimum(plane + 1, 2 * pairs - 1))
    low_ok = jnp.where(plane > 0, 1.0, 0.0).astype(F32)
    high_ok = jnp.where(plane < 2 * pairs - 1, 1.0, 0.0).astype(F32)

    def brick(j, x, p):
        slot = chip ^ chip_of(j & 7)
        value = jnp.where((j >> 3) == half, img_a_ref[slot, x, p], img_b_ref[slot, x, p])
        return value.astype(F32)

    depth = img_a_ref.shape[3]
    for x in range(rows):
        total = terms_ref[0, x].astype(F32)
        for k in range(1, pairs):
            total += terms_ref[k, x].astype(F32)
        pieces = []
        for p in range(2):
            low = brick(below, x, p)[depth - 8 :] * low_ok
            own = img_a_ref[0, x, p].astype(F32)
            high = brick(above, x, p)[:8] * high_ok
            pieces.append(jnp.concatenate([low, own, high], axis=0)[4 : 4 + WIN])
        out_ref[x] = (jnp.concatenate(pieces, axis=0) - total).astype(BF16)
        for p in range(2):
            grad_ref[x, p] = total[p * WIN + 4 : p * WIN + 4 + depth]


def start_brick(place, terms, img_a, img_b):
    _, rows, height, n = terms.shape
    return pl.pallas_call(
        start_kernel,
        in_specs=[SMEM, VMEM, VMEM, VMEM],
        out_specs=[VMEM, VMEM],
        out_shape=[
            jax.ShapeDtypeStruct((rows, height, n), BF16),
            jax.ShapeDtypeStruct((rows, *img_a.shape[2:]), F32),
        ],
        compiler_params=pltpu.CompilerParams(vmem_limit_bytes=16 << 20),
        name="start_brick",
    )(place, terms, img_a, img_b)


def shifted(value, column):
    n = value.shape[1]
    before = jnp.where(column == 0, 0.0, pltpu.roll(value, 1, 1))
    after = jnp.where(column == n - 1, 0.0, pltpu.roll(value, n - 1, 1))
    return before, value, after


def conv_kernel(place_ref, low_ref, own_ref, high_ref, grad_ref, w1_ref, w2_ref, w3_ref, out_ref,
                cols_ref, a1_ref, a2_ref):
    rows, height, n = own_ref.shape
    hid = 32
    ext = 3 * rows
    brick, plane = (place_ref[1], place_ref[2])
    flag = lambda ok: jnp.where(ok, 1.0, 0.0).astype(F32)
    x_low, x_high = (flag(brick > 0), flag(brick < 48 // rows - 1))
    z_low, z_high = (flag(plane > 0), flag(plane < 256 // 16 - 1))

    for x in range(ext):
        src = (low_ref, own_ref, high_ref)[x // rows]
        value = src[x % rows].astype(F32)
        column = lax.broadcasted_iota(jnp.int32, value.shape, 1)
        for d, part in enumerate(shifted(value, column)):
            at = (x * 3 + d) * height
            cols_ref[at : at + height] = part.astype(BF16)

    column1 = lax.broadcasted_iota(jnp.int32, (w1_ref.shape[0], n), 1)
    w1 = w1_ref[:, : 9 * height]
    for x in range(ext - 2):
        at = x * 3 * height
        value = jnp.maximum(dot(w1, cols_ref[at : at + 9 * height]), 0.0)
        if x < rows - 1:
            value = value * x_low
        if x >= 2 * rows - 1:
            value = value * x_high
        value = jnp.concatenate(
            [value[: 2 * hid] * z_low, value[2 * hid : -2 * hid], value[-2 * hid :] * z_high], axis=0
        )
        for d, part in enumerate(shifted(value, column1)):
            a1_ref[x, d] = part.astype(BF16)

    blocks = 3
    out2 = 6 * hid
    for k in range(blocks):
        parts = {}
        for x in range(ext - 2):
            first = 0 if x <= ext - 5 else x - (ext - 5)
            last = min(x, 2)
            cols = jnp.concatenate([a1_ref[x, d, k * out2 : k * out2 + 256] for d in range(3)], axis=0)
            value = dot(w2_ref[first * out2 : (last + 1) * out2], cols)
            for dx in range(first, last + 1):
                piece = value[(dx - first) * out2 : (dx - first + 1) * out2]
                at = x - dx
                parts[at] = piece if at not in parts else parts[at] + piece
            done = x - 2
            if done >= 0:
                value = jnp.maximum(parts.pop(done), 0.0)
                if done < rows - 2:
                    value = value * x_low
                if done >= 2 * rows - 2:
                    value = value * x_high
                if k == 0:
                    value = jnp.concatenate([value[:hid] * z_low, value[hid:]], axis=0)
                if k == blocks - 1:
                    value = jnp.concatenate([value[:-hid], value[-hid:] * z_high], axis=0)
                a2_ref[done, k * out2 : (k + 1) * out2] = value.astype(BF16)

    depth = 16
    size = 2 * depth
    w3 = w3_ref[:, :576]
    last3 = rows - 1
    terms = []
    for x in range(rows + 2):
        first, last = (max(x - last3, 0), min(x, 2))
        value = dot(w3[first * 3 * size : (last + 1) * 3 * size], a2_ref[x])
        terms.append((first, value))
    column3 = lax.broadcasted_iota(jnp.int32, (size, n), 1)
    for x in range(rows):
        sums = []
        for d in range(3):
            total = 0.0
            for dx in range(3):
                first, value = terms[x + dx]
                at = ((dx - first) * 3 + d) * size
                total = total + value[at : at + size]
            sums.append(total)
        value = sums[1] + jnp.where(column3 == 0, 0.0, pltpu.roll(sums[0], 1, 1))
        value = value + jnp.where(column3 == n - 1, 0.0, pltpu.roll(sums[2], n - 1, 1))
        for p in range(2):
            out_ref[x, p] = (value[p * depth : (p + 1) * depth] - grad_ref[x, p]).astype(BF16)


def regularized(place, low, own, high, grad, w1, w2, w3):
    rows, height, n = own.shape
    ext = 3 * rows
    return pl.pallas_call(
        conv_kernel,
        in_specs=[SMEM] + [VMEM] * 7,
        out_specs=VMEM,
        out_shape=jax.ShapeDtypeStruct(grad.shape, BF16),
        scratch_shapes=[
            pltpu.VMEM((ext * 3 * height, n), BF16),
            pltpu.VMEM((ext - 2, 3, 640, n), BF16),
            pltpu.VMEM((ext - 4, 576, n), BF16),
        ],
        compiler_params=pltpu.CompilerParams(vmem_limit_bytes=40 << 20),
        cost_estimate=pl.CostEstimate(flops=6 << 30, bytes_accessed=4 << 20, transcendentals=0),
        name="regularized",
    )(place, low, own, high, grad, w1, w2, w3)


def weights_kernel(b1_ref, b2_ref, b3_ref, w1_ref, w2_ref, w3_ref):
    base = b1_ref[...].astype(F32)
    for a in range(20):
        moved = base if a == 0 else pltpu.roll(base, a, 1)
        w1_ref[a * 32 : (a + 1) * 32] = moved.astype(BF16)
    for dx in range(3):
        for dy in range(3):
            base = b2_ref[dx * 3 + dy].astype(F32)
            for a in range(6):
                moved = base if a == 0 else pltpu.roll(base, a * 32, 1)
                at = (dx * 6 + a) * 32
                w2_ref[at : at + 32, dy * 256 : (dy + 1) * 256] = moved.astype(BF16)
    base = b3_ref[...].astype(F32)
    for t in range(18):
        row = jnp.broadcast_to(base[t : t + 1], (16, base.shape[1]))
        moved = pltpu.roll(row, 0, 1, stride=16, stride_axis=0)
        moved = pltpu.roll(moved, 0, 1, stride=16, stride_axis=0)
        w3_ref[t * 16 : (t + 1) * 16] = moved.astype(BF16)


def banded_weights(conv_in, conv_mid, conv_out):
    b1 = jnp.pad(conv_in.transpose(0, 2, 4, 1, 3), ((0, 0),) * 4 + ((1, WIN - 4),))
    b1 = jnp.pad(b1.reshape(32, 18 * WIN), ((0, 0), (0, 512 - 18 * WIN)))
    b2 = conv_mid.transpose(2, 4, 0, 3, 1).reshape(9, 32, 96)
    b2 = jnp.pad(b2, ((0, 0), (0, 0), (0, 160)))
    b3 = conv_out.transpose(2, 4, 0, 3, 1).reshape(18, 96)
    b3 = jnp.pad(b3, ((0, 0), (0, 640 - 96)))
    return pl.pallas_call(
        weights_kernel,
        in_specs=[VMEM] * 3,
        out_specs=[VMEM] * 3,
        out_shape=[
            jax.ShapeDtypeStruct((640, 512), BF16),
            jax.ShapeDtypeStruct((576, 768), BF16),
            jax.ShapeDtypeStruct((288, 640), BF16),
        ],
        compiler_params=pltpu.CompilerParams(vmem_limit_bytes=16 << 20),
        name="banded_weights",
    )(b1, b2, b3)


def gathered(brick, chips):
    hop = lambda v, k: lax.ppermute(v, "coil", [(i, i ^ (2 * k)) for i in range(2 * chips)])
    held = jnp.stack([brick] + [hop(brick, k) for k in (2, 4, 6)])
    return jnp.stack([held, hop(held, 1)], axis=1).reshape(-1, *brick.shape)


def step(image, sensitivity, kspace, sampling, conv_in, conv_mid, conv_out):
    rows, parts, depth, n = image.shape
    coils, slabs = (lax.axis_size("coil"), lax.axis_size("slab"))
    coil, slab = (lax.axis_index("coil"), lax.axis_index("slab"))
    place = jnp.stack([coil, slab, plane_of(coil)]).astype(jnp.int32)
    pairs = coils // 2
    chips = [[2 * i + c for i in range(pairs)] for c in range(2)]
    partner = [(i, i ^ 1) for i in range(coils)]
    there = [(a, b, coil_of(b)) for a in range(coils) for b in range(slabs)]
    across = [(a * slabs + b, c * slabs + a) for a, b, c in there]
    w1, w2, w3 = banded_weights(conv_in, conv_mid, conv_out)

    brick = lax.ppermute(image.astype(BF16), ("coil", "slab"), across)
    sens = lax.all_to_all(
        sensitivity[0].reshape(slabs, rows, parts, depth, n), "slab", 0, 0, tiled=True
    )
    img_a = gathered(brick, pairs)
    img_b = lax.ppermute(img_a, "coil", partner)

    kept, sent = coil_terms(place, sens, img_a, img_b, kspace[0], sampling, table(n))
    terms = pair_sum(kept, lax.ppermute(sent, "coil", partner))
    terms = lax.all_to_all(terms, "coil", 0, 0, tiled=True, axis_index_groups=chips)
    start, grad = start_brick(place, terms, img_a, img_b)

    up = [(i, i + 1) for i in range(slabs - 1)]
    low = lax.ppermute(start, "slab", up)
    high = lax.ppermute(start, "slab", [(j, i) for i, j in up])
    change = regularized(place, low, start, high, grad, w1, w2, w3)
    change = lax.ppermute(
        change, ("coil", "slab"), [(c * slabs + a, a * slabs + b) for a, b, c in there]
    )
    return image + change.astype(F32)


def solution(mesh):
    return jax.shard_map(
        step,
        mesh=mesh,
        in_specs=(
            P("coil", None, "slab", None),
            P("coil", None, None, "slab", None),
            P("coil", "slab", None, None, None),
            P(),
            P(),
            P(),
            P(),
        ),
        out_specs=P("coil", None, "slab", None),
        check_vma=False,
    )
```
